32 devices in a mesh: groups: 2 (over x), query: 8 (over z, y), target: 2 (over core).
Axes of the slice: x: 2, y: 2, z: 4, core: 2. Of those that a mesh axis runs over, the one named last changes fastest.
Arguments:
- query_input: bfloat16 [32, 960, 128], P(('groups', 'query')), parts along dimension 0, may hold values from -18 to 18
- target_input: bfloat16 [64, 960, 128], P(('groups', 'query', 'target')), parts along dimension 0, may hold values from -18 to 18
- conv_weight: bfloat16 [3, 3, 128, 128], replicated, may hold values from -0.1875 to 0.1875
- conv_bias: float32 [128], replicated, may hold values from -3 to 3
Outputs:
- flow: float32 [2, 16, 480], P(None, ('groups', 'query')), parts along dimension 1
The draws below stay inside these ranges and needn't reach their ends.
There are 2 independent parts, one for each index of `groups`. The reference program is written for one: setup_inputs(seed, part) draws one part's arguments, and reference() takes and returns one part's arrays. A program takes and returns all parts, laid end to end along the dimension named above; an argument that names none is the same for every part. Nothing has to cross between parts.
All inputs are finite; a program needn't handle non-finite values.
Results may differ from the reference program's by a relative error of at most 0.0026.
Values may be sent and summed in bfloat16 or wider, within the bound.
A program may use at most 64 MiB of HBM per device.

```python
import math
import jax
import jax.numpy as jnp
from jax import lax

C = 128
CIN = 128
W = 480
QUERY_ROWS = 8
TARGET_ROWS = 16


def draw_frames(key):
    folded = jax.random.fold_in(key, 4111)
    key_query, key_target = jax.random.split(folded, 2)
    query_shape = (2 * QUERY_ROWS, 2 * W, CIN)
    target_shape = (2 * TARGET_ROWS, 2 * W, CIN)
    queries = jnp.clip(jax.random.normal(key_query, query_shape, jnp.float32), -6.0, 6.0)
    targets = jnp.clip(jax.random.normal(key_target, target_shape, jnp.float32), -6.0, 6.0)
    return (queries, targets)


def draw_query_input(key, part):
    return draw_frames(key)[0].astype(jnp.bfloat16)


def draw_target_input(key, part):
    return draw_frames(key)[1].astype(jnp.bfloat16)


def noise(own_key, shape, deviation, limit, held_as=jnp.bfloat16):
    values = deviation * jax.random.normal(own_key, shape, jnp.float32)
    return jnp.clip(values, min=-limit, max=limit).astype(held_as)


def setup_inputs(seed: int = 0, part: int = 0) -> dict:
    key_of = jax.random.split(jax.random.key(seed), 5)
    own_keys = jax.random.split(jax.random.fold_in(key_of[4], part), 5)
    query_input = draw_query_input(jax.random.fold_in(jax.random.fold_in(key_of[4], part), 71), part)
    target_input = draw_target_input(jax.random.fold_in(jax.random.fold_in(key_of[4], part), 71), part)
    conv_weight = noise(key_of[2], (3, 3, CIN, C), (9 * CIN) ** -0.5, 0.1875)
    conv_bias = noise(key_of[3], (C,), 0.5, 3.0, jnp.float32)
    return dict(query_input=query_input, target_input=target_input, conv_weight=conv_weight, conv_bias=conv_bias)


CELL = 0.0625

def convolve(frame, conv_weight, conv_bias):
    padded = jnp.pad(frame, ((1, 0), (1, 0), (0, 0)))
    out_rows = frame.shape[0] // 2
    out_cols = frame.shape[1] // 2
    channels = frame.shape[2]
    summed = jnp.zeros((out_rows * out_cols, conv_weight.shape[3]), jnp.float32)
    for tap_row in range(3):
        for tap_col in range(3):
            window = padded[tap_row:tap_row + 2 * out_rows:2, tap_col:tap_col + 2 * out_cols:2]
            summed = summed + jnp.dot(window.reshape(out_rows * out_cols, channels), conv_weight[tap_row, tap_col], preferred_element_type=jnp.float32)
    return (summed + conv_bias).astype(jnp.bfloat16)

def reference(query_input, target_input, conv_weight, conv_bias):
    queries = convolve(query_input, conv_weight, conv_bias)
    targets = convolve(target_input, conv_weight, conv_bias)
    positions = jnp.arange(TARGET_ROWS * W, dtype=jnp.int32)
    target_x = (positions % W).astype(jnp.float32) * CELL
    target_y = (positions // W).astype(jnp.float32) * CELL
    inv_root = 1.0 / math.sqrt(C)

    def match(band_queries):
        scores = jnp.dot(band_queries, targets.T, preferred_element_type=jnp.float32) * inv_root
        highest = lax.optimization_barrier(jnp.max(scores, axis=1, keepdims=True))
        weights = jnp.exp(scores - highest)
        weight_sum = lax.optimization_barrier(jnp.sum(weights, axis=1))
        sum_x = jnp.dot(weights, target_x, precision=lax.Precision.HIGHEST)
        sum_y = jnp.dot(weights, target_y, precision=lax.Precision.HIGHEST)
        return (sum_x / weight_sum, sum_y / weight_sum)
    mean_x, mean_y = lax.map(match, queries.reshape(QUERY_ROWS, W, C))
    query_x = jnp.arange(W, dtype=jnp.int32).astype(jnp.float32)[None, :] * CELL
    query_y = jnp.arange(QUERY_ROWS, dtype=jnp.int32).astype(jnp.float32)[:, None] * CELL
    return jnp.stack([mean_x - query_x, mean_y - query_y])
```

```python
import functools
import math

import jax
import jax.numpy as jnp
from jax import lax
from jax.experimental import pallas as pl
from jax.experimental.pallas import tpu as pltpu
from jax.sharding import PartitionSpec as P

CELL = 0.0625
MESH = pl.DeviceIdType.MESH
MEMBERS = 4
PAD = 8


def kernel(
    queries_total,
    cores,
    q_hbm,
    t_hbm,
    w_hbm,
    bias_hbm,
    out_ref,
    q_in,
    t_in,
    w_ref,
    bias_ref,
    load,
    spread,
    rim_q_out,
    rim_t_out,
    rim_q_in,
    rim_t_in,
    q_all,
    t_all,
    stats_out,
    stats_in,
    rim_send,
    rim_recv,
    q_send,
    q_recv,
    t_send,
    t_recv,
    s_send,
    s_recv,
):
    n = queries_total
    members = MEMBERS
    cols = n // members
    width = t_in.shape[1] // 2
    half = width // cores
    channels = w_ref.shape[2]
    q = lax.axis_index("query")
    c = lax.axis_index("target")
    other = 1 - c
    member = q // cols
    col = q % cols
    share = q * cores + c

    def target(query, core):
        return {"query": query, "target": core}

    barrier = pltpu.get_barrier_semaphore()
    near = [(True, q, other)]
    near += [(q > 0, q - 1, c), (q < n - 1, q + 1, c)]
    near += [((c == 0) & (q > 0), q - 1, other), ((c == 1) & (q < n - 1), q + 1, other)]
    near += [(member > 0, q - cols, c), (member < members - 1, q + cols, c)]
    near += [(True, member * cols + (col + d) % cols, c) for d in range(1, cols)]
    expected = 0
    for present, query, core in near:
        if present is True:
            pl.semaphore_signal(
                barrier, inc=1, device_id=target(query, core), device_id_type=MESH
            )
            expected = expected + 1
        else:

            @pl.when(present)
            def _(query=query, core=core):
                pl.semaphore_signal(
                    barrier, inc=1, device_id=target(query, core), device_id_type=MESH
                )

            expected = expected + present.astype(jnp.int32)

    loads = [
        pltpu.make_async_copy(source, buffer, load.at[index])
        for index, (source, buffer) in enumerate(
            [
                (q_hbm.at[1], q_in.at[1]),
                (t_hbm.at[1], t_in.at[1]),
                (w_hbm.at[0], w_ref.at[0]),
                (q_hbm.at[0], q_in.at[0]),
                (t_hbm.at[0], t_in.at[0]),
                (w_hbm.at[1], w_ref.at[1]),
                (w_hbm.at[2], w_ref.at[2]),
                (bias_hbm, bias_ref),
            ]
        )
    ]
    for copy in loads:
        copy.start()

    for slot in range(4):
        spread[slot, 0:PAD, :] = jnp.zeros((PAD, spread.shape[2]), jnp.float32)

    def taps(slot, first, count):
        parts = [
            spread[slot, pl.ds(PAD - 1 + tap + 2 * first, count, stride=2), :] for tap in range(3)
        ]
        return jnp.concatenate(parts, axis=1).astype(jnp.bfloat16)

    def dot(a, b):
        return jnp.dot(a, b, preferred_element_type=jnp.float32)

    for copy in loads[:3]:
        copy.wait()
    spread[0, PAD:, :] = q_in[1].astype(jnp.float32)
    spread[1, PAD:, :] = t_in[1].astype(jnp.float32)
    first = pl.multiple_of(c * half, 8)
    q_low = taps(0, first, half)
    t_low = taps(1, 0, width)
    rim_q_out[...] = dot(q_low, w_ref[0]).astype(jnp.bfloat16)
    rim_t_out[...] = dot(t_low, w_ref[0]).astype(jnp.bfloat16)

    for copy in loads[3:]:
        copy.wait()
    spread[2, PAD:, :] = q_in[0].astype(jnp.float32)
    spread[3, PAD:, :] = t_in[0].astype(jnp.float32)
    q_sum = dot(q_low, w_ref[2]) + dot(taps(2, first, half), w_ref[1]) + bias_ref[...]
    t_sum = dot(t_low, w_ref[2]) + dot(taps(3, 0, width), w_ref[1]) + bias_ref[...]

    pl.semaphore_wait(barrier, expected)

    def rim_copies():
        following = share + 1
        return (
            pltpu.make_async_remote_copy(
                src_ref=rim_q_out,
                dst_ref=rim_q_in,
                send_sem=rim_send.at[0],
                recv_sem=rim_recv.at[0],
                device_id=target(q + 1, c),
                device_id_type=MESH,
            ),
            pltpu.make_async_remote_copy(
                src_ref=rim_t_out,
                dst_ref=rim_t_in,
                send_sem=rim_send.at[1],
                recv_sem=rim_recv.at[1],
                device_id=target(following // cores, following % cores),
                device_id_type=MESH,
            ),
        )

    rim_q_copy, rim_t_copy = rim_copies()

    @pl.when(q < n - 1)
    def _():
        rim_q_copy.start()

    @pl.when(share < n * cores - 1)
    def _():
        rim_t_copy.start()

    @pl.when(q > 0)
    def _():
        rim_q_copy.wait_recv()

    @pl.when(q == 0)
    def _():
        rim_q_in[...] = jnp.zeros(rim_q_in.shape, jnp.bfloat16)

    scale = math.log2(math.e) / math.sqrt(channels)
    q_all[member] = ((q_sum + rim_q_in[...].astype(jnp.float32)) * scale).astype(jnp.bfloat16)

    halves = [(0, half // 32 * 16), (half // 32 * 16, half - half // 32 * 16)]

    def q_copy(tile, part, upward):
        place, size = halves[part]
        return pltpu.make_async_remote_copy(
            src_ref=q_all.at[tile, pl.ds(place, size)],
            dst_ref=q_all.at[tile, pl.ds(place, size)],
            send_sem=q_send.at[1 if upward else 0, tile, part],
            recv_sem=q_recv.at[tile, part],
            device_id=target(q + cols if upward else q - cols, c),
            device_id_type=MESH,
        )

    def goes(tile, upward):
        if upward:
            return (tile <= member) & (member < members - 1)
        return (tile >= member) & (member > 0)

    def tile_at(step):
        short = jnp.minimum(member, members - 1 - member)
        apart = (step + 1) // 2
        both = member - apart if step % 2 else member + apart
        rest = jnp.where(
            member < members - 1 - member, member + (step - short), member - (step - short)
        )
        return jnp.where(step <= 2 * short, both, rest)

    def pass_on(tile, part):
        for upward in (False, True):

            @pl.when(goes(tile, upward))
            def _(upward=upward):
                q_copy(tile, part, upward).start()

    def take(step):
        tile = tile_at(step)
        for part in range(2):
            q_copy(tile, part, True).wait_recv()
            pass_on(tile, part)

    for part in range(2):
        pass_on(member, part)

    @pl.when(share > 0)
    def _():
        rim_t_copy.wait_recv()

    @pl.when(share == 0)
    def _():
        rim_t_in[...] = jnp.zeros(rim_t_in.shape, jnp.bfloat16)

    t_all[0] = (t_sum + rim_t_in[...].astype(jnp.float32)).astype(jnp.bfloat16)

    def t_copy(d):
        return pltpu.make_async_remote_copy(
            src_ref=t_all.at[0],
            dst_ref=t_all.at[2 * d],
            send_sem=t_send.at[2 * d],
            recv_sem=t_recv.at[2 * d],
            device_id=target(member * cols + (col + d) % cols, c),
            device_id_type=MESH,
        )

    def t_forward(d):
        return pltpu.make_async_remote_copy(
            src_ref=t_all.at[2 * d],
            dst_ref=t_all.at[2 * d + 1],
            send_sem=t_send.at[2 * d + 1],
            recv_sem=t_recv.at[2 * d + 1],
            device_id=target(q, other),
            device_id_type=MESH,
        )

    for d in range(1, cols):
        t_copy(d).start()
    t_forward(0).start()

    row = lax.broadcasted_iota(jnp.int32, (PAD, width), 0)
    place = lax.broadcasted_iota(jnp.int32, (PAD, width), 1) - width // 2
    values = jnp.where(row == 0, 1, jnp.where(row == 1, place, 0)).astype(jnp.bfloat16)

    def piece(tile, slot):
        scores = lax.dot_general(
            t_all[slot], q_all[tile], (((1,), (1,)), ((), ())), preferred_element_type=jnp.float32
        )
        top = jnp.max(scores, axis=0, keepdims=True)
        weights = jnp.exp2(scores - top).astype(jnp.bfloat16)
        sums = dot(values, weights)
        source = member * cols + (col - slot // 2 + cols) % cols
        core = c if slot % 2 == 0 else other
        height = (source * cores + core).astype(jnp.float32) * CELL
        total = sums[0:1]
        return (top, total, sums[1:2] * CELL, total * height)

    def joined(parts):
        top = functools.reduce(jnp.maximum, [part[0] for part in parts])
        scales = [jnp.exp2(part[0] - top) for part in parts]
        return (top,) + tuple(
            functools.reduce(
                jnp.add, [part[index] * factor for part, factor in zip(parts, scales)]
            )
            for index in range(1, 4)
        )

    def s_copy(tile, step, away):
        return pltpu.make_async_remote_copy(
            src_ref=stats_out.at[step],
            dst_ref=stats_in.at[c, member],
            send_sem=s_send.at[step, away],
            recv_sem=s_recv.at[c, member],
            device_id=target(tile * cols + col, c if away == 0 else other),
            device_id_type=MESH,
        )

    def s_arrival(tile, core):
        return pltpu.make_async_remote_copy(
            src_ref=stats_out.at[0],
            dst_ref=stats_in.at[core, tile],
            send_sem=s_send.at[0, 0],
            recv_sem=s_recv.at[core, tile],
            device_id=target(q, other),
            device_id_type=MESH,
        )

    def finish(step, parts):
        tile = member if step == 0 else tile_at(step)
        state = joined(parts)
        for index in range(4):
            stats_out[step, index : index + 1, 0:half] = state[index]
            if step == 0:
                stats_in[c, member, index : index + 1, 0:half] = state[index]
        for away in range(2):
            if step > 0 or away == 1:
                s_copy(tile, step, away).start()

    parts = [piece(member, 0)]
    t_forward(0).wait_recv()
    parts.append(piece(member, 1))
    take(1)
    take(2)
    for d in range(1, cols):
        t_copy(d).wait_recv()
        t_forward(d).start()
    for d in range(1, cols):
        parts.append(piece(member, 2 * d))
    for d in range(1, cols):
        t_forward(d).wait_recv()
        parts.append(piece(member, 2 * d + 1))
    finish(0, parts)
    for step in range(1, members):
        if step > 2:
            take(step)
        finish(step, [piece(tile_at(step), slot) for slot in range(2 * cols)])

    s_arrival(member, other).wait_recv()
    for step in range(1, members):
        for core in range(cores):
            s_arrival(tile_at(step), core).wait_recv()

    for core in range(cores):
        state = joined(
            [
                tuple(stats_in[core, k, index : index + 1, 0:half] for index in range(4))
                for k in range(members)
            ]
        )
        out_ref[0, :, core * half : (core + 1) * half] = state[2] / state[1]
        out_ref[1, :, core * half : (core + 1) * half] = state[3] / state[1]

    @pl.when(q < n - 1)
    def _():
        rim_q_copy.wait_send()

    @pl.when(share < n * cores - 1)
    def _():
        rim_t_copy.wait_send()

    for step in range(members):
        tile = member if step == 0 else tile_at(step)
        for part in range(2):
            for upward in (False, True):

                @pl.when(goes(tile, upward))
                def _(tile=tile, part=part, upward=upward):
                    q_copy(tile, part, upward).wait_send()

    for d in range(1, cols):
        t_copy(d).wait_send()
    for d in range(cols):
        t_forward(d).wait_send()
    for step in range(members):
        tile = member if step == 0 else tile_at(step)
        for away in range(2):
            if step > 0 or away == 1:
                s_copy(tile, step, away).wait_send()


def on_device(query_input, target_input, conv_weight, conv_bias):
    n = lax.axis_size("query")
    cores = lax.axis_size("target")
    cols = n // MEMBERS
    width = target_input.shape[1] // 2
    half = width // cores
    channels = conv_weight.shape[3]
    depth = conv_weight.shape[2]
    assert query_input.shape[0] == 2 and target_input.shape[0] == 2
    assert cores == 2 and n % MEMBERS == 0
    weight = conv_weight.reshape(3, 3 * depth, channels)
    bf16 = jnp.bfloat16
    means = pl.pallas_call(
        functools.partial(kernel, n, cores),
        out_shape=jax.ShapeDtypeStruct((2, 1, width), jnp.float32),
        in_specs=[pl.BlockSpec(memory_space=pl.ANY)] * 4,
        out_specs=pl.BlockSpec(memory_space=pltpu.VMEM),
        scratch_shapes=[
            pltpu.VMEM((2, 2 * width, depth), bf16),
            pltpu.VMEM((2, 2 * width, depth), bf16),
            pltpu.VMEM((3, 3 * depth, channels), bf16),
            pltpu.VMEM((1, channels), jnp.float32),
            pltpu.SemaphoreType.DMA((8,)),
            pltpu.VMEM((4, PAD + 2 * width, depth), jnp.float32),
            pltpu.VMEM((half, channels), bf16),
            pltpu.VMEM((width, channels), bf16),
            pltpu.VMEM((half, channels), bf16),
            pltpu.VMEM((width, channels), bf16),
            pltpu.VMEM((MEMBERS, half, channels), bf16),
            pltpu.VMEM((2 * cols, width, channels), bf16),
            pltpu.VMEM((MEMBERS, 8, 256), jnp.float32),
            pltpu.VMEM((cores, MEMBERS, 8, 256), jnp.float32),
            pltpu.SemaphoreType.DMA((2,)),
            pltpu.SemaphoreType.DMA((2,)),
            pltpu.SemaphoreType.DMA((2, MEMBERS, 2)),
            pltpu.SemaphoreType.DMA((MEMBERS, 2)),
            pltpu.SemaphoreType.DMA((2 * cols,)),
            pltpu.SemaphoreType.DMA((2 * cols,)),
            pltpu.SemaphoreType.DMA((MEMBERS, 2)),
            pltpu.SemaphoreType.DMA((2, MEMBERS)),
        ],
        compiler_params=pltpu.CompilerParams(collective_id=0, has_side_effects=True),
    )(query_input, target_input, weight, conv_bias.reshape(1, channels))
    column = lax.broadcasted_iota(jnp.int32, (2, 1, width), 2)
    axis = lax.broadcasted_iota(jnp.int32, (2, 1, width), 0)
    shift = jnp.where(axis == 0, column - width // 2, lax.axis_index("query"))
    return means - shift.astype(jnp.float32) * CELL


def solution(mesh):
    placed = (
        P(("groups", "query"), None, None),
        P(("groups", "query", "target"), None, None),
        P(),
        P(),
    )
    return jax.shard_map(
        on_device,
        mesh=mesh,
        in_specs=placed,
        out_specs=P(None, ("groups", "query"), None),
        check_vma=False,
    )
```

```python
import functools
import math

import jax
import jax.numpy as jnp
from jax import lax
from jax.experimental import pallas as pl
from jax.experimental.pallas import tpu as pltpu
from jax.sharding import PartitionSpec as P

CELL = 0.0625
MESH = pl.DeviceIdType.MESH
MEMBERS = 4
PAD = 8


def kernel(
    queries_total,
    cores,
    q_hbm,
    t_hbm,
    w_hbm,
    bias_hbm,
    out_ref,
    q_in,
    t_in,
    w_ref,
    bias_ref,
    load,
    spread,
    rim_q_out,
    rim_t_out,
    rim_q_in,
    rim_t_in,
    q_all,
    t_all,
    stats_out,
    stats_in,
    rim_send,
    rim_recv,
    q_send,
    q_recv,
    ready,
    t_send,
    t_recv,
    s_send,
    s_recv,
):
    n = queries_total
    members = MEMBERS
    cols = n // members
    width = t_in.shape[1] // 2
    half = width // cores
    channels = w_ref.shape[2]
    q = lax.axis_index("query")
    c = lax.axis_index("target")
    other = 1 - c
    member = q // cols
    col = q % cols
    share = q * cores + c

    def target(query, core):
        return {"query": query, "target": core}

    barrier = pltpu.get_barrier_semaphore()
    near = [(True, q, other)]
    near += [(q > 0, q - 1, c), (q < n - 1, q + 1, c)]
    near += [((c == 0) & (q > 0), q - 1, other), ((c == 1) & (q < n - 1), q + 1, other)]
    near += [(member > 0, q - cols, c), (member < members - 1, q + cols, c)]
    near += [(True, member * cols + (col + d) % cols, c) for d in range(1, cols)]
    expected = 0
    for present, query, core in near:
        if present is True:
            pl.semaphore_signal(
                barrier, inc=1, device_id=target(query, core), device_id_type=MESH
            )
            expected = expected + 1
        else:

            @pl.when(present)
            def _(query=query, core=core):
                pl.semaphore_signal(
                    barrier, inc=1, device_id=target(query, core), device_id_type=MESH
                )

            expected = expected + present.astype(jnp.int32)

    loads = [
        pltpu.make_async_copy(source, buffer, load.at[index])
        for index, (source, buffer) in enumerate(
            [
                (q_hbm.at[1], q_in.at[1]),
                (t_hbm.at[1], t_in.at[1]),
                (w_hbm.at[0], w_ref.at[0]),
                (q_hbm.at[0], q_in.at[0]),
                (t_hbm.at[0], t_in.at[0]),
                (w_hbm.at[1], w_ref.at[1]),
                (w_hbm.at[2], w_ref.at[2]),
                (bias_hbm, bias_ref),
            ]
        )
    ]
    for copy in loads:
        copy.start()

    for slot in range(4):
        spread[slot, 0:PAD, :] = jnp.zeros((PAD, spread.shape[2]), jnp.float32)

    def taps(slot, first, count):
        parts = [
            spread[slot, pl.ds(PAD - 1 + tap + 2 * first, count, stride=2), :] for tap in range(3)
        ]
        return jnp.concatenate(parts, axis=1).astype(jnp.bfloat16)

    def dot(a, b):
        return jnp.dot(a, b, preferred_element_type=jnp.float32)

    for copy in loads[:3]:
        copy.wait()
    spread[0, PAD:, :] = q_in[1].astype(jnp.float32)
    spread[1, PAD:, :] = t_in[1].astype(jnp.float32)
    first = pl.multiple_of(c * half, 8)
    q_low = taps(0, first, half)
    t_low = taps(1, 0, width)
    rim_q_out[...] = dot(q_low, w_ref[0]).astype(jnp.bfloat16)
    rim_t_out[...] = dot(t_low, w_ref[0]).astype(jnp.bfloat16)

    for copy in loads[3:]:
        copy.wait()
    spread[2, PAD:, :] = q_in[0].astype(jnp.float32)
    spread[3, PAD:, :] = t_in[0].astype(jnp.float32)
    q_sum = dot(q_low, w_ref[2]) + dot(taps(2, first, half), w_ref[1]) + bias_ref[...]
    t_sum = dot(t_low, w_ref[2]) + dot(taps(3, 0, width), w_ref[1]) + bias_ref[...]

    pl.semaphore_wait(barrier, expected)

    def rim_copies():
        following = share + 1
        return (
            pltpu.make_async_remote_copy(
                src_ref=rim_q_out,
                dst_ref=rim_q_in,
                send_sem=rim_send.at[0],
                recv_sem=rim_recv.at[0],
                device_id=target(q + 1, c),
                device_id_type=MESH,
            ),
            pltpu.make_async_remote_copy(
                src_ref=rim_t_out,
                dst_ref=rim_t_in,
                send_sem=rim_send.at[1],
                recv_sem=rim_recv.at[1],
                device_id=target(following // cores, following % cores),
                device_id_type=MESH,
            ),
        )

    rim_q_copy, rim_t_copy = rim_copies()

    @pl.when(q < n - 1)
    def _():
        rim_q_copy.start()

    @pl.when(share < n * cores - 1)
    def _():
        rim_t_copy.start()

    for turn in range(members - 2):

        @pl.when(member < members - 1)
        def _(turn=turn):
            pl.semaphore_signal(
                ready.at[turn, 0], inc=1, device_id=target(q + cols, c), device_id_type=MESH
            )

        @pl.when(member > 0)
        def _(turn=turn):
            pl.semaphore_signal(
                ready.at[turn, 1], inc=1, device_id=target(q - cols, c), device_id_type=MESH
            )
            pl.semaphore_wait(ready.at[turn, 0], 1)

        @pl.when(member < members - 1)
        def _(turn=turn):
            pl.semaphore_wait(ready.at[turn, 1], 1)

    @pl.when(q > 0)
    def _():
        rim_q_copy.wait_recv()

    @pl.when(q == 0)
    def _():
        rim_q_in[...] = jnp.zeros(rim_q_in.shape, jnp.bfloat16)

    scale = math.log2(math.e) / math.sqrt(channels)
    q_all[member] = ((q_sum + rim_q_in[...].astype(jnp.float32)) * scale).astype(jnp.bfloat16)

    def tile_at(step):
        short = jnp.minimum(member, members - 1 - member)
        apart = (step + 1) // 2
        both = member - apart if step % 2 else member + apart
        rest = jnp.where(
            member < members - 1 - member, member + (step - short), member - (step - short)
        )
        return jnp.where(step <= 2 * short, both, rest)

    def q_copy(step):
        return pltpu.make_async_remote_copy(
            src_ref=q_all.at[member],
            dst_ref=q_all.at[member],
            send_sem=q_send.at[step],
            recv_sem=q_recv.at[member],
            device_id=target(tile_at(step) * cols + col, c),
            device_id_type=MESH,
        )

    def take(step):
        pltpu.make_async_remote_copy(
            src_ref=q_all.at[member],
            dst_ref=q_all.at[tile_at(step)],
            send_sem=q_send.at[step],
            recv_sem=q_recv.at[tile_at(step)],
            device_id=target(tile_at(step) * cols + col, c),
            device_id_type=MESH,
        ).wait_recv()

    for step in range(members - 1, 0, -1):
        q_copy(step).start()

    @pl.when(share > 0)
    def _():
        rim_t_copy.wait_recv()

    @pl.when(share == 0)
    def _():
        rim_t_in[...] = jnp.zeros(rim_t_in.shape, jnp.bfloat16)

    t_all[0] = (t_sum + rim_t_in[...].astype(jnp.float32)).astype(jnp.bfloat16)

    def t_copy(d):
        return pltpu.make_async_remote_copy(
            src_ref=t_all.at[0],
            dst_ref=t_all.at[2 * d],
            send_sem=t_send.at[2 * d],
            recv_sem=t_recv.at[2 * d],
            device_id=target(member * cols + (col + d) % cols, c),
            device_id_type=MESH,
        )

    def t_forward(d):
        return pltpu.make_async_remote_copy(
            src_ref=t_all.at[2 * d],
            dst_ref=t_all.at[2 * d + 1],
            send_sem=t_send.at[2 * d + 1],
            recv_sem=t_recv.at[2 * d + 1],
            device_id=target(q, other),
            device_id_type=MESH,
        )

    for d in range(1, cols):
        t_copy(d).start()
    t_forward(0).start()

    row = lax.broadcasted_iota(jnp.int32, (PAD, width), 0)
    place = lax.broadcasted_iota(jnp.int32, (PAD, width), 1) - width // 2
    values = jnp.where(row == 0, 1, jnp.where(row == 1, place, 0)).astype(jnp.bfloat16)

    def piece(tile, slot):
        scores = lax.dot_general(
            t_all[slot], q_all[tile], (((1,), (1,)), ((), ())), preferred_element_type=jnp.float32
        )
        top = jnp.max(scores, axis=0, keepdims=True)
        weights = jnp.exp2(scores - top).astype(jnp.bfloat16)
        sums = dot(values, weights)
        source = member * cols + (col - slot // 2 + cols) % cols
        core = c if slot % 2 == 0 else other
        height = (source * cores + core).astype(jnp.float32) * CELL
        total = sums[0:1]
        return (top, total, sums[1:2] * CELL, total * height)

    def joined(parts):
        top = functools.reduce(jnp.maximum, [part[0] for part in parts])
        scales = [jnp.exp2(part[0] - top) for part in parts]
        return (top,) + tuple(
            functools.reduce(
                jnp.add, [part[index] * factor for part, factor in zip(parts, scales)]
            )
            for index in range(1, 4)
        )

    def s_copy(tile, step, away):
        return pltpu.make_async_remote_copy(
            src_ref=stats_out.at[step],
            dst_ref=stats_in.at[c, member],
            send_sem=s_send.at[step, away],
            recv_sem=s_recv.at[c, member],
            device_id=target(tile * cols + col, c if away == 0 else other),
            device_id_type=MESH,
        )

    def s_arrival(tile, core):
        return pltpu.make_async_remote_copy(
            src_ref=stats_out.at[0],
            dst_ref=stats_in.at[core, tile],
            send_sem=s_send.at[0, 0],
            recv_sem=s_recv.at[core, tile],
            device_id=target(q, other),
            device_id_type=MESH,
        )

    def finish(step, parts):
        tile = member if step == 0 else tile_at(step)
        state = joined(parts)
        for index in range(4):
            stats_out[step, index : index + 1, 0:half] = state[index]
            if step == 0:
                stats_in[c, member, index : index + 1, 0:half] = state[index]
        for away in range(2):
            if step > 0 or away == 1:
                s_copy(tile, step, away).start()

    tiles = [member] + [tile_at(step) for step in range(1, members)]
    parts = [[piece(member, 0)]] + [[] for _ in range(1, members)]
    t_forward(0).wait_recv()
    parts[0].append(piece(member, 1))
    take(1)
    parts[1] += [piece(tiles[1], slot) for slot in range(2)]
    for d in range(1, cols):
        t_copy(d).wait_recv()
        t_forward(d).start()
    for step in range(2):
        parts[step] += [piece(tiles[step], 2 * d) for d in range(1, cols)]
    take(2)
    parts[2] += [piece(tiles[2], slot) for slot in range(2 * cols) if slot < 2 or slot % 2 == 0]
    for d in range(1, cols):
        t_forward(d).wait_recv()
    for step in range(3):
        parts[step] += [piece(tiles[step], 2 * d + 1) for d in range(1, cols)]
        finish(step, parts[step])
    for step in range(3, members):
        take(step)
        finish(step, [piece(tiles[step], slot) for slot in range(2 * cols)])

    s_arrival(member, other).wait_recv()
    for step in range(1, members):
        for core in range(cores):
            s_arrival(tile_at(step), core).wait_recv()

    for core in range(cores):
        state = joined(
            [
                tuple(stats_in[core, k, index : index + 1, 0:half] for index in range(4))
                for k in range(members)
            ]
        )
        out_ref[0, :, core * half : (core + 1) * half] = state[2] / state[1]
        out_ref[1, :, core * half : (core + 1) * half] = state[3] / state[1]

    @pl.when(q < n - 1)
    def _():
        rim_q_copy.wait_send()

    @pl.when(share < n * cores - 1)
    def _():
        rim_t_copy.wait_send()

    for step in range(1, members):
        q_copy(step).wait_send()
    for d in range(1, cols):
        t_copy(d).wait_send()
    for d in range(cols):
        t_forward(d).wait_send()
    for step in range(members):
        tile = member if step == 0 else tile_at(step)
        for away in range(2):
            if step > 0 or away == 1:
                s_copy(tile, step, away).wait_send()


def on_device(query_input, target_input, conv_weight, conv_bias):
    n = lax.axis_size("query")
    cores = lax.axis_size("target")
    cols = n // MEMBERS
    width = target_input.shape[1] // 2
    half = width // cores
    channels = conv_weight.shape[3]
    depth = conv_weight.shape[2]
    assert query_input.shape[0] == 2 and target_input.shape[0] == 2
    assert cores == 2 and n % MEMBERS == 0
    weight = conv_weight.reshape(3, 3 * depth, channels)
    bf16 = jnp.bfloat16
    means = pl.pallas_call(
        functools.partial(kernel, n, cores),
        out_shape=jax.ShapeDtypeStruct((2, 1, width), jnp.float32),
        in_specs=[pl.BlockSpec(memory_space=pl.ANY)] * 4,
        out_specs=pl.BlockSpec(memory_space=pltpu.VMEM),
        scratch_shapes=[
            pltpu.VMEM((2, 2 * width, depth), bf16),
            pltpu.VMEM((2, 2 * width, depth), bf16),
            pltpu.VMEM((3, 3 * depth, channels), bf16),
            pltpu.VMEM((1, channels), jnp.float32),
            pltpu.SemaphoreType.DMA((8,)),
            pltpu.VMEM((4, PAD + 2 * width, depth), jnp.float32),
            pltpu.VMEM((half, channels), bf16),
            pltpu.VMEM((width, channels), bf16),
            pltpu.VMEM((half, channels), bf16),
            pltpu.VMEM((width, channels), bf16),
            pltpu.VMEM((MEMBERS, half, channels), bf16),
            pltpu.VMEM((2 * cols, width, channels), bf16),
            pltpu.VMEM((MEMBERS, 8, 256), jnp.float32),
            pltpu.VMEM((cores, MEMBERS, 8, 256), jnp.float32),
            pltpu.SemaphoreType.DMA((2,)),
            pltpu.SemaphoreType.DMA((2,)),
            pltpu.SemaphoreType.DMA((MEMBERS,)),
            pltpu.SemaphoreType.DMA((MEMBERS,)),
            pltpu.SemaphoreType.REGULAR((MEMBERS - 2, 2)),
            pltpu.SemaphoreType.DMA((2 * cols,)),
            pltpu.SemaphoreType.DMA((2 * cols,)),
            pltpu.SemaphoreType.DMA((MEMBERS, 2)),
            pltpu.SemaphoreType.DMA((2, MEMBERS)),
        ],
        compiler_params=pltpu.CompilerParams(collective_id=0, has_side_effects=True),
    )(query_input, target_input, weight, conv_bias.reshape(1, channels))
    column = lax.broadcasted_iota(jnp.int32, (2, 1, width), 2)
    axis = lax.broadcasted_iota(jnp.int32, (2, 1, width), 0)
    shift = jnp.where(axis == 0, column - width // 2, lax.axis_index("query"))
    return means - shift.astype(jnp.float32) * CELL


def solution(mesh):
    placed = (
        P(("groups", "query"), None, None),
        P(("groups", "query", "target"), None, None),
        P(),
        P(),
    )
    return jax.shard_map(
        on_device,
        mesh=mesh,
        in_specs=placed,
        out_specs=P(None, ("groups", "query"), None),
        check_vma=False,
    )
```

```python
import functools
import math

import jax
import jax.numpy as jnp
from jax import lax
from jax.experimental import pallas as pl
from jax.experimental.pallas import tpu as pltpu
from jax.sharding import PartitionSpec as P

CELL = 0.0625
MESH = pl.DeviceIdType.MESH
MEMBERS = 4
PAD = 8


def kernel(
    queries_total,
    cores,
    q_hbm,
    t_hbm,
    w_hbm,
    bias_hbm,
    out_ref,
    q_in,
    t_in,
    w_ref,
    bias_ref,
    load,
    spread,
    rim_q_out,
    rim_t_out,
    rim_q_in,
    rim_t_in,
    q_all,
    t_all,
    stats_out,
    stats_in,
    rim_send,
    rim_recv,
    q_send,
    q_recv,
    ready,
    t_send,
    t_recv,
    s_send,
    s_recv,
):
    n = queries_total
    members = MEMBERS
    cols = n // members
    width = t_in.shape[1] // 2
    half = width // cores
    channels = w_ref.shape[2]
    q = lax.axis_index("query")
    c = lax.axis_index("target")
    other = 1 - c
    member = q // cols
    col = q % cols
    share = q * cores + c

    def target(query, core):
        return {"query": query, "target": core}

    barrier = pltpu.get_barrier_semaphore()
    near = [(True, q, other)]
    near += [(q > 0, q - 1, c), (q < n - 1, q + 1, c)]
    near += [((c == 0) & (q > 0), q - 1, other), ((c == 1) & (q < n - 1), q + 1, other)]
    near += [(member > 0, q - cols, c), (member < members - 1, q + cols, c)]
    near += [(True, member * cols + (col + d) % cols, c) for d in range(1, cols)]
    expected = 0
    for present, query, core in near:
        if present is True:
            pl.semaphore_signal(
                barrier, inc=1, device_id=target(query, core), device_id_type=MESH
            )
            expected = expected + 1
        else:

            @pl.when(present)
            def _(query=query, core=core):
                pl.semaphore_signal(
                    barrier, inc=1, device_id=target(query, core), device_id_type=MESH
                )

            expected = expected + present.astype(jnp.int32)

    loads = [
        pltpu.make_async_copy(source, buffer, load.at[index])
        for index, (source, buffer) in enumerate(
            [
                (q_hbm.at[1], q_in.at[1]),
                (t_hbm.at[1], t_in.at[1]),
                (w_hbm.at[0], w_ref.at[0]),
                (q_hbm.at[0], q_in.at[0]),
                (t_hbm.at[0], t_in.at[0]),
                (w_hbm.at[1], w_ref.at[1]),
                (w_hbm.at[2], w_ref.at[2]),
                (bias_hbm, bias_ref),
            ]
        )
    ]
    for copy in loads:
        copy.start()

    for slot in range(4):
        spread[slot, 0:PAD, :] = jnp.zeros((PAD, spread.shape[2]), jnp.float32)

    def taps(slot, first, count):
        parts = [
            spread[slot, pl.ds(PAD - 1 + tap + 2 * first, count, stride=2), :] for tap in range(3)
        ]
        return jnp.concatenate(parts, axis=1).astype(jnp.bfloat16)

    def dot(a, b):
        return jnp.dot(a, b, preferred_element_type=jnp.float32)

    for copy in loads[:3]:
        copy.wait()
    spread[0, PAD:, :] = q_in[1].astype(jnp.float32)
    spread[1, PAD:, :] = t_in[1].astype(jnp.float32)
    first = pl.multiple_of(c * half, 8)
    q_low = taps(0, first, half)
    t_low = taps(1, 0, width)
    rim_q_out[...] = dot(q_low, w_ref[0]).astype(jnp.bfloat16)
    rim_t_out[...] = dot(t_low, w_ref[0]).astype(jnp.bfloat16)

    for copy in loads[3:]:
        copy.wait()
    spread[2, PAD:, :] = q_in[0].astype(jnp.float32)
    spread[3, PAD:, :] = t_in[0].astype(jnp.float32)
    q_sum = dot(q_low, w_ref[2]) + dot(taps(2, first, half), w_ref[1]) + bias_ref[...]
    t_sum = dot(t_low, w_ref[2]) + dot(taps(3, 0, width), w_ref[1]) + bias_ref[...]

    pl.semaphore_wait(barrier, expected)

    def rim_copies():
        following = share + 1
        return (
            pltpu.make_async_remote_copy(
                src_ref=rim_q_out,
                dst_ref=rim_q_in,
                send_sem=rim_send.at[0],
                recv_sem=rim_recv.at[0],
                device_id=target(q + 1, c),
                device_id_type=MESH,
            ),
            pltpu.make_async_remote_copy(
                src_ref=rim_t_out,
                dst_ref=rim_t_in,
                send_sem=rim_send.at[1],
                recv_sem=rim_recv.at[1],
                device_id=target(following // cores, following % cores),
                device_id_type=MESH,
            ),
        )

    rim_q_copy, rim_t_copy = rim_copies()

    @pl.when(q < n - 1)
    def _():
        rim_q_copy.start()

    @pl.when(share < n * cores - 1)
    def _():
        rim_t_copy.start()

    def ready_signal(turn):
        @pl.when(member < members - 1)
        def _():
            pl.semaphore_signal(
                ready.at[turn, 0], inc=1, device_id=target(q + cols, c), device_id_type=MESH
            )

        @pl.when(member > 0)
        def _():
            pl.semaphore_signal(
                ready.at[turn, 1], inc=1, device_id=target(q - cols, c), device_id_type=MESH
            )

    def ready_wait(turn):
        @pl.when(member > 0)
        def _():
            pl.semaphore_wait(ready.at[turn, 0], 1)

        @pl.when(member < members - 1)
        def _():
            pl.semaphore_wait(ready.at[turn, 1], 1)

    ready_signal(0)

    @pl.when(q > 0)
    def _():
        rim_q_copy.wait_recv()

    @pl.when(q == 0)
    def _():
        rim_q_in[...] = jnp.zeros(rim_q_in.shape, jnp.bfloat16)

    scale = math.log2(math.e) / math.sqrt(channels)
    q_all[member] = ((q_sum + rim_q_in[...].astype(jnp.float32)) * scale).astype(jnp.bfloat16)

    def tile_at(step):
        short = jnp.minimum(member, members - 1 - member)
        apart = (step + 1) // 2
        both = member - apart if step % 2 else member + apart
        rest = jnp.where(
            member < members - 1 - member, member + (step - short), member - (step - short)
        )
        return jnp.where(step <= 2 * short, both, rest)

    def q_copy(apart, upward):
        return pltpu.make_async_remote_copy(
            src_ref=q_all.at[member],
            dst_ref=q_all.at[member],
            send_sem=q_send.at[1 if upward else 0, apart],
            recv_sem=q_recv.at[member],
            device_id=target(q + apart * cols if upward else q - apart * cols, c),
            device_id_type=MESH,
        )

    def q_each(apart, act):
        for upward in (False, True):

            @pl.when(member + apart < members if upward else member >= apart)
            def _(upward=upward):
                act(q_copy(apart, upward))

    def take(step):
        pltpu.make_async_remote_copy(
            src_ref=q_all.at[member],
            dst_ref=q_all.at[tile_at(step)],
            send_sem=q_send.at[0, step],
            recv_sem=q_recv.at[tile_at(step)],
            device_id=target(tile_at(step) * cols + col, c),
            device_id_type=MESH,
        ).wait_recv()

    q_each(1, lambda copy: copy.start())
    for apart in range(2, members - 1):
        ready_wait(apart - 2)
        ready_signal(apart - 1)
        q_each(apart, lambda copy: copy.start())

    @pl.when(share > 0)
    def _():
        rim_t_copy.wait_recv()

    @pl.when(share == 0)
    def _():
        rim_t_in[...] = jnp.zeros(rim_t_in.shape, jnp.bfloat16)

    t_all[0] = (t_sum + rim_t_in[...].astype(jnp.float32)).astype(jnp.bfloat16)

    def t_copy(d):
        return pltpu.make_async_remote_copy(
            src_ref=t_all.at[0],
            dst_ref=t_all.at[2 * d],
            send_sem=t_send.at[2 * d],
            recv_sem=t_recv.at[2 * d],
            device_id=target(member * cols + (col + d) % cols, c),
            device_id_type=MESH,
        )

    def t_forward(d):
        return pltpu.make_async_remote_copy(
            src_ref=t_all.at[2 * d],
            dst_ref=t_all.at[2 * d + 1],
            send_sem=t_send.at[2 * d + 1],
            recv_sem=t_recv.at[2 * d + 1],
            device_id=target(q, other),
            device_id_type=MESH,
        )

    for d in range(1, cols):
        t_copy(d).start()
    t_forward(0).start()
    ready_wait(members - 3)
    q_each(members - 1, lambda copy: copy.start())

    row = lax.broadcasted_iota(jnp.int32, (PAD, width), 0)
    place = lax.broadcasted_iota(jnp.int32, (PAD, width), 1) - width // 2
    values = jnp.where(row == 0, 1, jnp.where(row == 1, place, 0)).astype(jnp.bfloat16)

    def piece(tile, slot):
        scores = lax.dot_general(
            t_all[slot], q_all[tile], (((1,), (1,)), ((), ())), preferred_element_type=jnp.float32
        )
        top = jnp.max(scores, axis=0, keepdims=True)
        weights = jnp.exp2((scores - top).astype(jnp.bfloat16))
        sums = dot(values, weights)
        source = member * cols + (col - slot // 2 + cols) % cols
        core = c if slot % 2 == 0 else other
        height = (source * cores + core).astype(jnp.float32) * CELL
        total = sums[0:1]
        return (top, total, sums[1:2] * CELL, total * height)

    def joined(parts):
        top = functools.reduce(jnp.maximum, [part[0] for part in parts])
        scales = [jnp.exp2(part[0] - top) for part in parts]
        return (top,) + tuple(
            functools.reduce(
                jnp.add, [part[index] * factor for part, factor in zip(parts, scales)]
            )
            for index in range(1, 4)
        )

    def s_copy(tile, step, away):
        return pltpu.make_async_remote_copy(
            src_ref=stats_out.at[step],
            dst_ref=stats_in.at[c, member],
            send_sem=s_send.at[step, away],
            recv_sem=s_recv.at[c, member],
            device_id=target(tile * cols + col, c if away == 0 else other),
            device_id_type=MESH,
        )

    def s_arrival(tile, core):
        return pltpu.make_async_remote_copy(
            src_ref=stats_out.at[0],
            dst_ref=stats_in.at[core, tile],
            send_sem=s_send.at[0, 0],
            recv_sem=s_recv.at[core, tile],
            device_id=target(q, other),
            device_id_type=MESH,
        )

    def finish(step, parts):
        tile = member if step == 0 else tile_at(step)
        state = joined(parts)
        for index in range(4):
            stats_out[step, index : index + 1, 0:half] = state[index]
            if step == 0:
                stats_in[c, member, index : index + 1, 0:half] = state[index]
        for away in range(2):
            if step > 0 or away == 1:
                s_copy(tile, step, away).start()

    tiles = [member] + [tile_at(step) for step in range(1, members)]
    parts = [[piece(member, 0)]] + [[] for _ in range(1, members)]
    t_forward(0).wait_recv()
    parts[0].append(piece(member, 1))
    take(1)
    parts[1] += [piece(tiles[1], slot) for slot in range(2)]
    for d in range(1, cols):
        t_copy(d).wait_recv()
        t_forward(d).start()
    for step in range(2):
        parts[step] += [piece(tiles[step], 2 * d) for d in range(1, cols)]
    take(2)
    parts[2] += [piece(tiles[2], slot) for slot in range(2 * cols) if slot < 2 or slot % 2 == 0]
    for d in range(1, cols):
        t_forward(d).wait_recv()
    for step in range(3):
        parts[step] += [piece(tiles[step], 2 * d + 1) for d in range(1, cols)]
        finish(step, parts[step])
    for step in range(3, members):
        take(step)
        finish(step, [piece(tiles[step], slot) for slot in range(2 * cols)])

    s_arrival(member, other).wait_recv()
    for step in range(1, members):
        for core in range(cores):
            s_arrival(tile_at(step), core).wait_recv()

    for core in range(cores):
        state = joined(
            [
                tuple(stats_in[core, k, index : index + 1, 0:half] for index in range(4))
                for k in range(members)
            ]
        )
        out_ref[0, :, core * half : (core + 1) * half] = state[2] / state[1]
        out_ref[1, :, core * half : (core + 1) * half] = state[3] / state[1]

    @pl.when(q < n - 1)
    def _():
        rim_q_copy.wait_send()

    @pl.when(share < n * cores - 1)
    def _():
        rim_t_copy.wait_send()

    for apart in range(1, members):
        q_each(apart, lambda copy: copy.wait_send())
    for d in range(1, cols):
        t_copy(d).wait_send()
    for d in range(cols):
        t_forward(d).wait_send()
    for step in range(members):
        tile = member if step == 0 else tile_at(step)
        for away in range(2):
            if step > 0 or away == 1:
                s_copy(tile, step, away).wait_send()


def on_device(query_input, target_input, conv_weight, conv_bias):
    n = lax.axis_size("query")
    cores = lax.axis_size("target")
    cols = n // MEMBERS
    width = target_input.shape[1] // 2
    half = width // cores
    channels = conv_weight.shape[3]
    depth = conv_weight.shape[2]
    assert query_input.shape[0] == 2 and target_input.shape[0] == 2
    assert cores == 2 and n % MEMBERS == 0
    weight = conv_weight.reshape(3, 3 * depth, channels)
    bf16 = jnp.bfloat16
    means = pl.pallas_call(
        functools.partial(kernel, n, cores),
        out_shape=jax.ShapeDtypeStruct((2, 1, width), jnp.float32),
        in_specs=[pl.BlockSpec(memory_space=pl.ANY)] * 4,
        out_specs=pl.BlockSpec(memory_space=pltpu.VMEM),
        scratch_shapes=[
            pltpu.VMEM((2, 2 * width, depth), bf16),
            pltpu.VMEM((2, 2 * width, depth), bf16),
            pltpu.VMEM((3, 3 * depth, channels), bf16),
            pltpu.VMEM((1, channels), jnp.float32),
            pltpu.SemaphoreType.DMA((8,)),
            pltpu.VMEM((4, PAD + 2 * width, depth), jnp.float32),
            pltpu.VMEM((half, channels), bf16),
            pltpu.VMEM((width, channels), bf16),
            pltpu.VMEM((half, channels), bf16),
            pltpu.VMEM((width, channels), bf16),
            pltpu.VMEM((MEMBERS, half, channels), bf16),
            pltpu.VMEM((2 * cols, width, channels), bf16),
            pltpu.VMEM((MEMBERS, 4, 256), jnp.float32),
            pltpu.VMEM((cores, MEMBERS, 4, 256), jnp.float32),
            pltpu.SemaphoreType.DMA((2,)),
            pltpu.SemaphoreType.DMA((2,)),
            pltpu.SemaphoreType.DMA((2, MEMBERS)),
            pltpu.SemaphoreType.DMA((MEMBERS,)),
            pltpu.SemaphoreType.REGULAR((MEMBERS - 2, 2)),
            pltpu.SemaphoreType.DMA((2 * cols,)),
            pltpu.SemaphoreType.DMA((2 * cols,)),
            pltpu.SemaphoreType.DMA((MEMBERS, 2)),
            pltpu.SemaphoreType.DMA((2, MEMBERS)),
        ],
        compiler_params=pltpu.CompilerParams(collective_id=0, has_side_effects=True),
    )(query_input, target_input, weight, conv_bias.reshape(1, channels))
    column = lax.broadcasted_iota(jnp.int32, (2, 1, width), 2)
    axis = lax.broadcasted_iota(jnp.int32, (2, 1, width), 0)
    shift = jnp.where(axis == 0, column - width // 2, lax.axis_index("query"))
    return means - shift.astype(jnp.float32) * CELL


def solution(mesh):
    placed = (
        P(("groups", "query"), None, None),
        P(("groups", "query", "target"), None, None),
        P(),
        P(),
    )
    return jax.shard_map(
        on_device,
        mesh=mesh,
        in_specs=placed,
        out_specs=P(None, ("groups", "query"), None),
        check_vma=False,
    )
```

```python
import functools
import math

import jax
import jax.numpy as jnp
from jax import lax
from jax.experimental import pallas as pl
from jax.experimental.pallas import tpu as pltpu
from jax.sharding import PartitionSpec as P

CELL = 0.0625
MESH = pl.DeviceIdType.MESH
MEMBERS = 4
PAD = 8


def kernel(
    queries_total,
    cores,
    q_hbm,
    t_hbm,
    w_hbm,
    bias_hbm,
    out_ref,
    q_in,
    t_in,
    w_ref,
    bias_ref,
    load,
    spread,
    rim_q_out,
    rim_t_out,
    rim_q_in,
    rim_t_in,
    q_all,
    t_all,
    stats_out,
    stats_in,
    rim_send,
    rim_recv,
    q_send,
    q_recv,
    ready,
    t_send,
    t_recv,
    s_send,
    s_recv,
):
    n = queries_total
    members = MEMBERS
    cols = n // members
    width = t_in.shape[1] // 2
    half = width // cores
    channels = w_ref.shape[2]
    q = lax.axis_index("query")
    c = lax.axis_index("target")
    other = 1 - c
    member = q // cols
    col = q % cols
    share = q * cores + c

    def target(query, core):
        return {"query": query, "target": core}

    barrier = pltpu.get_barrier_semaphore()
    near = [(True, q, other)]
    near += [(q > 0, q - 1, c), (q < n - 1, q + 1, c)]
    near += [((c == 0) & (q > 0), q - 1, other), ((c == 1) & (q < n - 1), q + 1, other)]
    near += [(member > 0, q - cols, c), (member < members - 1, q + cols, c)]
    near += [(True, member * cols + (col + d) % cols, c) for d in range(1, cols)]
    expected = 0
    for present, query, core in near:
        if present is True:
            pl.semaphore_signal(
                barrier, inc=1, device_id=target(query, core), device_id_type=MESH
            )
            expected = expected + 1
        else:

            @pl.when(present)
            def _(query=query, core=core):
                pl.semaphore_signal(
                    barrier, inc=1, device_id=target(query, core), device_id_type=MESH
                )

            expected = expected + present.astype(jnp.int32)

    loads = [
        pltpu.make_async_copy(source, buffer, load.at[index])
        for index, (source, buffer) in enumerate(
            [
                (q_hbm.at[1], q_in.at[1]),
                (t_hbm.at[1], t_in.at[1]),
                (w_hbm.at[0], w_ref.at[0]),
                (q_hbm.at[0], q_in.at[0]),
                (t_hbm.at[0], t_in.at[0]),
                (w_hbm.at[1], w_ref.at[1]),
                (w_hbm.at[2], w_ref.at[2]),
                (bias_hbm, bias_ref),
            ]
        )
    ]
    for copy in loads:
        copy.start()

    for slot in range(4):
        spread[slot, 0:PAD, :] = jnp.zeros((PAD, spread.shape[2]), jnp.float32)

    def taps(slot, first, count):
        parts = [
            spread[slot, pl.ds(PAD - 1 + tap + 2 * first, count, stride=2), :] for tap in range(3)
        ]
        return jnp.concatenate(parts, axis=1).astype(jnp.bfloat16)

    def dot(a, b):
        return jnp.dot(a, b, preferred_element_type=jnp.float32)

    for copy in loads[:3]:
        copy.wait()
    spread[0, PAD:, :] = q_in[1].astype(jnp.float32)
    spread[1, PAD:, :] = t_in[1].astype(jnp.float32)
    first = pl.multiple_of(c * half, 8)
    q_low = taps(0, first, half)
    t_low = taps(1, 0, width)
    rim_q_out[...] = dot(q_low, w_ref[0]).astype(jnp.bfloat16)
    rim_t_out[...] = dot(t_low, w_ref[0]).astype(jnp.bfloat16)

    for copy in loads[3:]:
        copy.wait()
    spread[2, PAD:, :] = q_in[0].astype(jnp.float32)
    spread[3, PAD:, :] = t_in[0].astype(jnp.float32)
    q_sum = dot(q_low, w_ref[2]) + dot(taps(2, first, half), w_ref[1]) + bias_ref[...]
    t_sum = dot(t_low, w_ref[2]) + dot(taps(3, 0, width), w_ref[1]) + bias_ref[...]

    pl.semaphore_wait(barrier, expected)

    def rim_copies():
        following = share + 1
        return (
            pltpu.make_async_remote_copy(
                src_ref=rim_q_out,
                dst_ref=rim_q_in,
                send_sem=rim_send.at[0],
                recv_sem=rim_recv.at[0],
                device_id=target(q + 1, c),
                device_id_type=MESH,
            ),
            pltpu.make_async_remote_copy(
                src_ref=rim_t_out,
                dst_ref=rim_t_in,
                send_sem=rim_send.at[1],
                recv_sem=rim_recv.at[1],
                device_id=target(following // cores, following % cores),
                device_id_type=MESH,
            ),
        )

    rim_q_copy, rim_t_copy = rim_copies()

    @pl.when(q < n - 1)
    def _():
        rim_q_copy.start()

    @pl.when(share < n * cores - 1)
    def _():
        rim_t_copy.start()

    def ready_signal(turn):
        @pl.when(member < members - 1)
        def _():
            pl.semaphore_signal(
                ready.at[turn, 0], inc=1, device_id=target(q + cols, c), device_id_type=MESH
            )

        @pl.when(member > 0)
        def _():
            pl.semaphore_signal(
                ready.at[turn, 1], inc=1, device_id=target(q - cols, c), device_id_type=MESH
            )

    def ready_wait(turn):
        @pl.when(member > 0)
        def _():
            pl.semaphore_wait(ready.at[turn, 0], 1)

        @pl.when(member < members - 1)
        def _():
            pl.semaphore_wait(ready.at[turn, 1], 1)

    for turn in range(members - 2):
        ready_signal(turn)
        ready_wait(turn)

    @pl.when(q > 0)
    def _():
        rim_q_copy.wait_recv()

    @pl.when(q == 0)
    def _():
        rim_q_in[...] = jnp.zeros(rim_q_in.shape, jnp.bfloat16)

    scale = math.log2(math.e) / math.sqrt(channels)
    q_all[member] = ((q_sum + rim_q_in[...].astype(jnp.float32)) * scale).astype(jnp.bfloat16)

    def tile_at(step):
        short = jnp.minimum(member, members - 1 - member)
        apart = (step + 1) // 2
        both = member - apart if step % 2 else member + apart
        rest = jnp.where(
            member < members - 1 - member, member + (step - short), member - (step - short)
        )
        return jnp.where(step <= 2 * short, both, rest)

    def q_copy(apart, upward):
        return pltpu.make_async_remote_copy(
            src_ref=q_all.at[member],
            dst_ref=q_all.at[member],
            send_sem=q_send.at[1 if upward else 0, apart],
            recv_sem=q_recv.at[member],
            device_id=target(q + apart * cols if upward else q - apart * cols, c),
            device_id_type=MESH,
        )

    def q_each(apart, act):
        for upward in (False, True):

            @pl.when(member + apart < members if upward else member >= apart)
            def _(upward=upward):
                act(q_copy(apart, upward))

    def take(step):
        pltpu.make_async_remote_copy(
            src_ref=q_all.at[member],
            dst_ref=q_all.at[tile_at(step)],
            send_sem=q_send.at[0, step],
            recv_sem=q_recv.at[tile_at(step)],
            device_id=target(tile_at(step) * cols + col, c),
            device_id_type=MESH,
        ).wait_recv()

    for apart in range(members - 1, 0, -1):
        q_each(apart, lambda copy: copy.start())

    @pl.when(share > 0)
    def _():
        rim_t_copy.wait_recv()

    @pl.when(share == 0)
    def _():
        rim_t_in[...] = jnp.zeros(rim_t_in.shape, jnp.bfloat16)

    t_all[0] = (t_sum + rim_t_in[...].astype(jnp.float32)).astype(jnp.bfloat16)

    def t_copy(d):
        return pltpu.make_async_remote_copy(
            src_ref=t_all.at[0],
            dst_ref=t_all.at[2 * d],
            send_sem=t_send.at[2 * d],
            recv_sem=t_recv.at[2 * d],
            device_id=target(member * cols + (col + d) % cols, c),
            device_id_type=MESH,
        )

    def t_forward(d):
        return pltpu.make_async_remote_copy(
            src_ref=t_all.at[2 * d],
            dst_ref=t_all.at[2 * d + 1],
            send_sem=t_send.at[2 * d + 1],
            recv_sem=t_recv.at[2 * d + 1],
            device_id=target(q, other),
            device_id_type=MESH,
        )

    for d in range(1, cols):
        t_copy(d).start()
    t_forward(0).start()

    row = lax.broadcasted_iota(jnp.int32, (PAD, width), 0)
    place = lax.broadcasted_iota(jnp.int32, (PAD, width), 1) - width // 2
    values = jnp.where(row == 0, 1, jnp.where(row == 1, place, 0)).astype(jnp.bfloat16)

    def block(tile, slots):
        kept = [
            lax.dot_general(
                t_all[slot],
                q_all[tile],
                (((1,), (1,)), ((), ())),
                preferred_element_type=jnp.float32,
            )
            for slot in slots
        ]
        top = functools.reduce(
            jnp.maximum, [jnp.max(scores, axis=0, keepdims=True) for scores in kept]
        )
        total, sum_x, sum_y = 0.0, 0.0, 0.0
        for slot, scores in zip(slots, kept):
            sums = dot(values, jnp.exp2((scores - top).astype(jnp.bfloat16)))
            source = member * cols + (col - slot // 2 + cols) % cols
            core = c if slot % 2 == 0 else other
            height = (source * cores + core).astype(jnp.float32) * CELL
            total = total + sums[0:1]
            sum_x = sum_x + sums[1:2]
            sum_y = sum_y + sums[0:1] * height
        return (top, total, sum_x * CELL, sum_y)

    def joined(parts):
        top = functools.reduce(jnp.maximum, [part[0] for part in parts])
        scales = [jnp.exp2(part[0] - top) for part in parts]
        return (top,) + tuple(
            functools.reduce(
                jnp.add, [part[index] * factor for part, factor in zip(parts, scales)]
            )
            for index in range(1, 4)
        )

    def s_copy(tile, step, away):
        return pltpu.make_async_remote_copy(
            src_ref=stats_out.at[step],
            dst_ref=stats_in.at[c, member],
            send_sem=s_send.at[step, away],
            recv_sem=s_recv.at[c, member],
            device_id=target(tile * cols + col, c if away == 0 else other),
            device_id_type=MESH,
        )

    def s_arrival(tile, core):
        return pltpu.make_async_remote_copy(
            src_ref=stats_out.at[0],
            dst_ref=stats_in.at[core, tile],
            send_sem=s_send.at[0, 0],
            recv_sem=s_recv.at[core, tile],
            device_id=target(q, other),
            device_id_type=MESH,
        )

    def finish(step, parts):
        tile = member if step == 0 else tile_at(step)
        state = joined(parts)
        for index in range(4):
            stats_out[step, index : index + 1, 0:half] = state[index]
            if step == 0:
                stats_in[c, member, index : index + 1, 0:half] = state[index]
        for away in range(2):
            if step > 0 or away == 1:
                s_copy(tile, step, away).start()

    tiles = [member] + [tile_at(step) for step in range(1, members)]
    every = list(range(2 * cols))
    direct = every[2::2]
    handed = every[3::2]
    t_forward(0).wait_recv()
    own = [block(member, [0, 1])]
    for d in range(1, cols):
        t_copy(d).wait_recv()
        t_forward(d).start()
    own.append(block(member, direct))
    take(1)
    first_part = [block(tiles[1], [0, 1] + direct)]
    for d in range(1, cols):
        t_forward(d).wait_recv()
    finish(0, own + [block(member, handed)])
    finish(1, first_part + [block(tiles[1], handed)])
    for step in range(2, members):
        take(step)
        finish(step, [block(tiles[step], every)])

    s_arrival(member, other).wait_recv()
    for step in range(1, members):
        for core in range(cores):
            s_arrival(tile_at(step), core).wait_recv()

    for core in range(cores):
        state = joined(
            [
                tuple(stats_in[core, k, index : index + 1, 0:half] for index in range(4))
                for k in range(members)
            ]
        )
        out_ref[0, :, core * half : (core + 1) * half] = state[2] / state[1]
        out_ref[1, :, core * half : (core + 1) * half] = state[3] / state[1]

    @pl.when(q < n - 1)
    def _():
        rim_q_copy.wait_send()

    @pl.when(share < n * cores - 1)
    def _():
        rim_t_copy.wait_send()

    for apart in range(1, members):
        q_each(apart, lambda copy: copy.wait_send())
    for d in range(1, cols):
        t_copy(d).wait_send()
    for d in range(cols):
        t_forward(d).wait_send()
    for step in range(members):
        tile = member if step == 0 else tile_at(step)
        for away in range(2):
            if step > 0 or away == 1:
                s_copy(tile, step, away).wait_send()


def on_device(query_input, target_input, conv_weight, conv_bias):
    n = lax.axis_size("query")
    cores = lax.axis_size("target")
    cols = n // MEMBERS
    width = target_input.shape[1] // 2
    half = width // cores
    channels = conv_weight.shape[3]
    depth = conv_weight.shape[2]
    assert query_input.shape[0] == 2 and target_input.shape[0] == 2
    assert cores == 2 and n % MEMBERS == 0
    weight = conv_weight.reshape(3, 3 * depth, channels)
    bf16 = jnp.bfloat16
    means = pl.pallas_call(
        functools.partial(kernel, n, cores),
        out_shape=jax.ShapeDtypeStruct((2, 1, width), jnp.float32),
        in_specs=[pl.BlockSpec(memory_space=pl.ANY)] * 4,
        out_specs=pl.BlockSpec(memory_space=pltpu.VMEM),
        scratch_shapes=[
            pltpu.VMEM((2, 2 * width, depth), bf16),
            pltpu.VMEM((2, 2 * width, depth), bf16),
            pltpu.VMEM((3, 3 * depth, channels), bf16),
            pltpu.VMEM((1, channels), jnp.float32),
            pltpu.SemaphoreType.DMA((8,)),
            pltpu.VMEM((4, PAD + 2 * width, depth), jnp.float32),
            pltpu.VMEM((half, channels), bf16),
            pltpu.VMEM((width, channels), bf16),
            pltpu.VMEM((half, channels), bf16),
            pltpu.VMEM((width, channels), bf16),
            pltpu.VMEM((MEMBERS, half, channels), bf16),
            pltpu.VMEM((2 * cols, width, channels), bf16),
            pltpu.VMEM((MEMBERS, 4, 256), jnp.float32),
            pltpu.VMEM((cores, MEMBERS, 4, 256), jnp.float32),
            pltpu.SemaphoreType.DMA((2,)),
            pltpu.SemaphoreType.DMA((2,)),
            pltpu.SemaphoreType.DMA((2, MEMBERS)),
            pltpu.SemaphoreType.DMA((MEMBERS,)),
            pltpu.SemaphoreType.REGULAR((MEMBERS - 2, 2)),
            pltpu.SemaphoreType.DMA((2 * cols,)),
            pltpu.SemaphoreType.DMA((2 * cols,)),
            pltpu.SemaphoreType.DMA((MEMBERS, 2)),
            pltpu.SemaphoreType.DMA((2, MEMBERS)),
        ],
        compiler_params=pltpu.CompilerParams(collective_id=0, has_side_effects=True),
    )(query_input, target_input, weight, conv_bias.reshape(1, channels))
    column = lax.broadcasted_iota(jnp.int32, (2, 1, width), 2)
    axis = lax.broadcasted_iota(jnp.int32, (2, 1, width), 0)
    shift = jnp.where(axis == 0, column - width // 2, lax.axis_index("query"))
    return means - shift.astype(jnp.float32) * CELL


def solution(mesh):
    placed = (
        P(("groups", "query"), None, None),
        P(("groups", "query", "target"), None, None),
        P(),
        P(),
    )
    return jax.shard_map(
        on_device,
        mesh=mesh,
        in_specs=placed,
        out_specs=P(None, ("groups", "query"), None),
        check_vma=False,
    )
```

```python
import functools
import math

import jax
import jax.numpy as jnp
from jax import lax
from jax.experimental import pallas as pl
from jax.experimental.pallas import tpu as pltpu
from jax.sharding import PartitionSpec as P

CELL = 0.0625
MESH = pl.DeviceIdType.MESH
MEMBERS = 4
PAD = 8


def kernel(
    queries_total,
    cores,
    q_hbm,
    t_hbm,
    w_hbm,
    bias_hbm,
    out_ref,
    q_in,
    t_in,
    w_ref,
    bias_ref,
    load,
    spread,
    rim_q_out,
    rim_t_out,
    rim_q_in,
    rim_t_in,
    q_all,
    t_all,
    stats_out,
    stats_in,
    rim_send,
    rim_recv,
    q_send,
    q_recv,
    ready,
    t_send,
    t_recv,
    s_send,
    s_recv,
):
    n = queries_total
    members = MEMBERS
    cols = n // members
    width = t_in.shape[1] // 2
    half = width // cores
    channels = w_ref.shape[2]
    q = lax.axis_index("query")
    c = lax.axis_index("target")
    other = 1 - c
    member = q // cols
    col = q % cols
    share = q * cores + c

    def target(query, core):
        return {"query": query, "target": core}

    barrier = pltpu.get_barrier_semaphore()
    near = [(True, q, other)]
    near += [(q > 0, q - 1, c), (q < n - 1, q + 1, c)]
    near += [((c == 0) & (q > 0), q - 1, other), ((c == 1) & (q < n - 1), q + 1, other)]
    near += [(member > 0, q - cols, c), (member < members - 1, q + cols, c)]
    near += [(True, member * cols + (col + d) % cols, c) for d in range(1, cols)]
    expected = 0
    for present, query, core in near:
        if present is True:
            pl.semaphore_signal(
                barrier, inc=1, device_id=target(query, core), device_id_type=MESH
            )
            expected = expected + 1
        else:

            @pl.when(present)
            def _(query=query, core=core):
                pl.semaphore_signal(
                    barrier, inc=1, device_id=target(query, core), device_id_type=MESH
                )

            expected = expected + present.astype(jnp.int32)

    loads = [
        pltpu.make_async_copy(source, buffer, load.at[index])
        for index, (source, buffer) in enumerate(
            [
                (q_hbm.at[1], q_in.at[1]),
                (t_hbm.at[1], t_in.at[1]),
                (w_hbm.at[0], w_ref.at[0]),
                (q_hbm.at[0], q_in.at[0]),
                (t_hbm.at[0], t_in.at[0]),
                (w_hbm.at[1], w_ref.at[1]),
                (w_hbm.at[2], w_ref.at[2]),
                (bias_hbm, bias_ref),
            ]
        )
    ]
    for copy in loads:
        copy.start()

    for slot in range(4):
        spread[slot, 0:PAD, :] = jnp.zeros((PAD, spread.shape[2]), jnp.float32)

    def taps(slot, first, count):
        parts = [
            spread[slot, pl.ds(PAD - 1 + tap + 2 * first, count, stride=2), :] for tap in range(3)
        ]
        return jnp.concatenate(parts, axis=1).astype(jnp.bfloat16)

    def dot(a, b):
        return jnp.dot(a, b, preferred_element_type=jnp.float32)

    for copy in loads[:3]:
        copy.wait()
    spread[0, PAD:, :] = q_in[1].astype(jnp.float32)
    spread[1, PAD:, :] = t_in[1].astype(jnp.float32)
    first = pl.multiple_of(c * half, 8)
    q_low = taps(0, first, half)
    t_low = taps(1, 0, width)
    rim_q_out[...] = dot(q_low, w_ref[0]).astype(jnp.bfloat16)
    rim_t_out[...] = dot(t_low, w_ref[0]).astype(jnp.bfloat16)

    for copy in loads[3:]:
        copy.wait()
    spread[2, PAD:, :] = q_in[0].astype(jnp.float32)
    spread[3, PAD:, :] = t_in[0].astype(jnp.float32)
    q_sum = dot(q_low, w_ref[2]) + dot(taps(2, first, half), w_ref[1]) + bias_ref[...]
    t_sum = dot(t_low, w_ref[2]) + dot(taps(3, 0, width), w_ref[1]) + bias_ref[...]

    pl.semaphore_wait(barrier, expected)

    def rim_copies():
        following = share + 1
        return (
            pltpu.make_async_remote_copy(
                src_ref=rim_q_out,
                dst_ref=rim_q_in,
                send_sem=rim_send.at[0],
                recv_sem=rim_recv.at[0],
                device_id=target(q + 1, c),
                device_id_type=MESH,
            ),
            pltpu.make_async_remote_copy(
                src_ref=rim_t_out,
                dst_ref=rim_t_in,
                send_sem=rim_send.at[1],
                recv_sem=rim_recv.at[1],
                device_id=target(following // cores, following % cores),
                device_id_type=MESH,
            ),
        )

    rim_q_copy, rim_t_copy = rim_copies()

    @pl.when(q < n - 1)
    def _():
        rim_q_copy.start()

    @pl.when(share < n * cores - 1)
    def _():
        rim_t_copy.start()

    def ready_signal(turn):
        @pl.when(member < members - 1)
        def _():
            pl.semaphore_signal(
                ready.at[turn, 0], inc=1, device_id=target(q + cols, c), device_id_type=MESH
            )

        @pl.when(member > 0)
        def _():
            pl.semaphore_signal(
                ready.at[turn, 1], inc=1, device_id=target(q - cols, c), device_id_type=MESH
            )

    def ready_wait(turn):
        @pl.when(member > 0)
        def _():
            pl.semaphore_wait(ready.at[turn, 0], 1)

        @pl.when(member < members - 1)
        def _():
            pl.semaphore_wait(ready.at[turn, 1], 1)

    for turn in range(members - 2):
        ready_signal(turn)
        ready_wait(turn)

    @pl.when(q > 0)
    def _():
        rim_q_copy.wait_recv()

    @pl.when(q == 0)
    def _():
        rim_q_in[...] = jnp.zeros(rim_q_in.shape, jnp.bfloat16)

    scale = math.log2(math.e) / math.sqrt(channels)
    q_all[member] = ((q_sum + rim_q_in[...].astype(jnp.float32)) * scale).astype(jnp.bfloat16)

    def tile_at(step):
        short = jnp.minimum(member, members - 1 - member)
        apart = (step + 1) // 2
        both = member - apart if step % 2 else member + apart
        rest = jnp.where(
            member < members - 1 - member, member + (step - short), member - (step - short)
        )
        return jnp.where(step <= 2 * short, both, rest)

    def q_copy(apart, upward):
        return pltpu.make_async_remote_copy(
            src_ref=q_all.at[member],
            dst_ref=q_all.at[member],
            send_sem=q_send.at[1 if upward else 0, apart],
            recv_sem=q_recv.at[member],
            device_id=target(q + apart * cols if upward else q - apart * cols, c),
            device_id_type=MESH,
        )

    def q_each(apart, act):
        for upward in (False, True):

            @pl.when(member + apart < members if upward else member >= apart)
            def _(upward=upward):
                act(q_copy(apart, upward))

    def take(step):
        pltpu.make_async_remote_copy(
            src_ref=q_all.at[member],
            dst_ref=q_all.at[tile_at(step)],
            send_sem=q_send.at[0, step],
            recv_sem=q_recv.at[tile_at(step)],
            device_id=target(tile_at(step) * cols + col, c),
            device_id_type=MESH,
        ).wait_recv()

    for apart in range(members - 1, 0, -1):
        q_each(apart, lambda copy: copy.start())

    @pl.when(share > 0)
    def _():
        rim_t_copy.wait_recv()

    @pl.when(share == 0)
    def _():
        rim_t_in[...] = jnp.zeros(rim_t_in.shape, jnp.bfloat16)

    t_all[0] = (t_sum + rim_t_in[...].astype(jnp.float32)).astype(jnp.bfloat16)

    def t_copy(d):
        return pltpu.make_async_remote_copy(
            src_ref=t_all.at[0],
            dst_ref=t_all.at[2 * d],
            send_sem=t_send.at[2 * d],
            recv_sem=t_recv.at[2 * d],
            device_id=target(member * cols + (col + d) % cols, c),
            device_id_type=MESH,
        )

    def t_forward(d):
        return pltpu.make_async_remote_copy(
            src_ref=t_all.at[2 * d],
            dst_ref=t_all.at[2 * d + 1],
            send_sem=t_send.at[2 * d + 1],
            recv_sem=t_recv.at[2 * d + 1],
            device_id=target(q, other),
            device_id_type=MESH,
        )

    for d in range(1, cols):
        t_copy(d).start()
    t_forward(0).start()

    row = lax.broadcasted_iota(jnp.int32, (PAD, width), 0)
    place = lax.broadcasted_iota(jnp.int32, (PAD, width), 1) - width // 2
    values = jnp.where(row == 0, 1, jnp.where(row == 1, place, 0)).astype(jnp.bfloat16)

    def block(tile, slots):
        kept = [
            lax.dot_general(
                t_all[slot],
                q_all[tile],
                (((1,), (1,)), ((), ())),
                preferred_element_type=jnp.float32,
            )
            for slot in slots
        ]
        top = functools.reduce(
            jnp.maximum, [jnp.max(scores, axis=0, keepdims=True) for scores in kept]
        )
        total, sum_x, sum_y = 0.0, 0.0, 0.0
        for slot, scores in zip(slots, kept):
            sums = dot(values, jnp.exp2((scores - top).astype(jnp.bfloat16)))
            source = member * cols + (col - slot // 2 + cols) % cols
            core = c if slot % 2 == 0 else other
            height = (source * cores + core).astype(jnp.float32) * CELL
            total = total + sums[0:1]
            sum_x = sum_x + sums[1:2]
            sum_y = sum_y + sums[0:1] * height
        return (top, total, sum_x * CELL, sum_y)

    def joined(parts):
        top = functools.reduce(jnp.maximum, [part[0] for part in parts])
        scales = [jnp.exp2(part[0] - top) for part in parts]
        return (top,) + tuple(
            functools.reduce(
                jnp.add, [part[index] * factor for part, factor in zip(parts, scales)]
            )
            for index in range(1, 4)
        )

    def s_copy(tile, step, away):
        return pltpu.make_async_remote_copy(
            src_ref=stats_out.at[step],
            dst_ref=stats_in.at[c, member],
            send_sem=s_send.at[step, away],
            recv_sem=s_recv.at[c, member],
            device_id=target(tile * cols + col, c if away == 0 else other),
            device_id_type=MESH,
        )

    def s_arrival(tile, core):
        return pltpu.make_async_remote_copy(
            src_ref=stats_out.at[0],
            dst_ref=stats_in.at[core, tile],
            send_sem=s_send.at[0, 0],
            recv_sem=s_recv.at[core, tile],
            device_id=target(q, other),
            device_id_type=MESH,
        )

    def finish(step, parts):
        tile = member if step == 0 else tile_at(step)
        state = joined(parts)
        for index in range(4):
            stats_out[step, index : index + 1, 0:half] = state[index]
            if step == 0:
                stats_in[c, member, index : index + 1, 0:half] = state[index]
        for away in range(2):
            if step > 0 or away == 1:
                s_copy(tile, step, away).start()

    tiles = [member] + [tile_at(step) for step in range(1, members)]
    every = list(range(2 * cols))
    direct = every[2::2]
    handed = every[3::2]
    t_forward(0).wait_recv()
    own = [block(member, [0, 1])]
    for d in range(1, cols):
        t_copy(d).wait_recv()
        t_forward(d).start()
    own.append(block(member, direct))
    last = members - 1
    take(last)
    first_part = [block(tiles[last], [0, 1] + direct)]
    for d in range(1, cols):
        t_forward(d).wait_recv()
    finish(last, first_part + [block(tiles[last], handed)])
    for step in range(last - 1, 0, -1):
        take(step)
        finish(step, [block(tiles[step], every)])
    finish(0, own + [block(member, handed)])

    s_arrival(member, other).wait_recv()
    for step in range(1, members):
        for core in range(cores):
            s_arrival(tile_at(step), core).wait_recv()

    for core in range(cores):
        state = joined(
            [
                tuple(stats_in[core, k, index : index + 1, 0:half] for index in range(4))
                for k in range(members)
            ]
        )
        out_ref[0, :, core * half : (core + 1) * half] = state[2] / state[1]
        out_ref[1, :, core * half : (core + 1) * half] = state[3] / state[1]

    @pl.when(q < n - 1)
    def _():
        rim_q_copy.wait_send()

    @pl.when(share < n * cores - 1)
    def _():
        rim_t_copy.wait_send()

    for apart in range(1, members):
        q_each(apart, lambda copy: copy.wait_send())
    for d in range(1, cols):
        t_copy(d).wait_send()
    for d in range(cols):
        t_forward(d).wait_send()
    for step in range(members):
        tile = member if step == 0 else tile_at(step)
        for away in range(2):
            if step > 0 or away == 1:
                s_copy(tile, step, away).wait_send()


def on_device(query_input, target_input, conv_weight, conv_bias):
    n = lax.axis_size("query")
    cores = lax.axis_size("target")
    cols = n // MEMBERS
    width = target_input.shape[1] // 2
    half = width // cores
    channels = conv_weight.shape[3]
    depth = conv_weight.shape[2]
    assert query_input.shape[0] == 2 and target_input.shape[0] == 2
    assert cores == 2 and n % MEMBERS == 0
    weight = conv_weight.reshape(3, 3 * depth, channels)
    bf16 = jnp.bfloat16
    means = pl.pallas_call(
        functools.partial(kernel, n, cores),
        out_shape=jax.ShapeDtypeStruct((2, 1, width), jnp.float32),
        in_specs=[pl.BlockSpec(memory_space=pl.ANY)] * 4,
        out_specs=pl.BlockSpec(memory_space=pltpu.VMEM),
        scratch_shapes=[
            pltpu.VMEM((2, 2 * width, depth), bf16),
            pltpu.VMEM((2, 2 * width, depth), bf16),
            pltpu.VMEM((3, 3 * depth, channels), bf16),
            pltpu.VMEM((1, channels), jnp.float32),
            pltpu.SemaphoreType.DMA((8,)),
            pltpu.VMEM((4, PAD + 2 * width, depth), jnp.float32),
            pltpu.VMEM((half, channels), bf16),
            pltpu.VMEM((width, channels), bf16),
            pltpu.VMEM((half, channels), bf16),
            pltpu.VMEM((width, channels), bf16),
            pltpu.VMEM((MEMBERS, half, channels), bf16),
            pltpu.VMEM((2 * cols, width, channels), bf16),
            pltpu.VMEM((MEMBERS, 4, 256), jnp.float32),
            pltpu.VMEM((cores, MEMBERS, 4, 256), jnp.float32),
            pltpu.SemaphoreType.DMA((2,)),
            pltpu.SemaphoreType.DMA((2,)),
            pltpu.SemaphoreType.DMA((2, MEMBERS)),
            pltpu.SemaphoreType.DMA((MEMBERS,)),
            pltpu.SemaphoreType.REGULAR((MEMBERS - 2, 2)),
            pltpu.SemaphoreType.DMA((2 * cols,)),
            pltpu.SemaphoreType.DMA((2 * cols,)),
            pltpu.SemaphoreType.DMA((MEMBERS, 2)),
            pltpu.SemaphoreType.DMA((2, MEMBERS)),
        ],
        compiler_params=pltpu.CompilerParams(collective_id=0, has_side_effects=True),
    )(query_input, target_input, weight, conv_bias.reshape(1, channels))
    column = lax.broadcasted_iota(jnp.int32, (2, 1, width), 2)
    axis = lax.broadcasted_iota(jnp.int32, (2, 1, width), 0)
    shift = jnp.where(axis == 0, column - width // 2, lax.axis_index("query"))
    return means - shift.astype(jnp.float32) * CELL


def solution(mesh):
    placed = (
        P(("groups", "query"), None, None),
        P(("groups", "query", "target"), None, None),
        P(),
        P(),
    )
    return jax.shard_map(
        on_device,
        mesh=mesh,
        in_specs=placed,
        out_specs=P(None, ("groups", "query"), None),
        check_vma=False,
    )
```
